32 devices in a mesh: seq: 8 (over z, x), head: 4 (over y, core).
Axes of the slice: x: 2, y: 2, z: 4, core: 2. Of those that a mesh axis runs over, the one named last changes fastest.
Arguments:
- queries: bfloat16 [9216, 32, 128], P(('seq', 'head')), may hold values from -4 to 4
- key_states: bfloat16 [9216, 4, 128], P(('seq', 'head')), may hold values from -4 to 4
- value_states: bfloat16 [9216, 4, 128], P(('seq', 'head')), may hold values from -6 to 6
- outputs: bfloat16 [9216, 32, 128], P(('seq', 'head')), may hold values from -6 to 6
- output_grad: bfloat16 [9216, 32, 128], P(('seq', 'head')), may hold values from -96 to 96
- logsumexp: float32 [9216, 32], P(('seq', 'head')), may hold values from 6.8 to 7.8
- random_owner: int32 [72, 3], replicated, may hold values from 0 to 7, all different within a row; in each aligned block of 9 rows (0 to 8, 9 to 17, ...) at most 4 rows name the same one
- random_slot: int32 [72, 3], replicated, may hold values from 0 to 8
Outputs:
- query_grad: bfloat16 [9216, 32, 128], P(('seq', 'head'))
- key_grad: bfloat16 [9216, 4, 128], P(('seq', 'head'))
- value_grad: bfloat16 [9216, 4, 128], P(('seq', 'head'))
The draws below stay inside these ranges and needn't reach their ends.
Inputs may be any that keep to these rules, and one draw needn't show every extreme that they name: `random_owner`: each row names 3 different indices. Within the 9 rows of one index of seq (aligned blocks of 9 rows), no index of seq appears more than 4 times, and some index appears exactly 4 times in some block.
All inputs are finite; a program needn't handle non-finite values.
Results may differ from the reference program's by a relative error of at most 0.005.
Values may be sent and summed in bfloat16 or wider, within the bound.
A program may use at most 128 MiB of HBM per device.

```python
import math
import jax
import jax.numpy as jnp
import numpy as np
from jax import lax

QH = 32
KVH = 4
HD = 128
BLK = 128
G = 2
RND = 3
TOKENS = 9216
NB = 72
QB = 9
MOST = 4
N_SEQ = 8


def bounded_field(key, field_shape):
    return jnp.clip(jax.random.normal(key, field_shape, jnp.float32), -4.0, 4.0)


def draw_queries(key, part):
    return bounded_field(jax.random.fold_in(key, 11), (TOKENS, QH, HD)).astype(jnp.bfloat16)


def draw_key_states(key, part):
    return bounded_field(jax.random.fold_in(key, 23), (TOKENS, KVH, HD)).astype(jnp.bfloat16)


def set_ends(array, own_key, smallest, top_value):
    extent = array.shape
    spot = [jax.random.randint(jax.random.fold_in(own_key, axis), (), 0, extent[axis]) for axis in range(len(extent))]
    array = array.at[tuple(spot)].set(smallest)
    longest = extent.index(max(extent))
    spot[longest] = (spot[longest] + 1) % extent[longest]
    return array.at[tuple(spot)].set(top_value)


def block_levels(own_key, dims, cuts, smallest, high):
    level = 1.0
    for dim, blocks in cuts:
        draws = jax.random.uniform(jax.random.fold_in(jax.random.fold_in(own_key, 6), dim), (blocks,), jnp.float32, smallest / len(cuts), high / len(cuts))
        level = level * jnp.repeat(jnp.exp(draws), dims[dim] // blocks).reshape((-1,) + (1,) * (len(dims) - 1 - dim))
    return level


def shared_out(stream_key, own, number, rows, amount, top, most, lean):
    ranking = jax.random.permutation(stream_key, amount)
    heavy_load, ordinary = load_shares(amount, rows * top, most, lean, True), load_shares(amount, rows * top, most, lean, False)
    places = jnp.arange(amount)

    def named(tallies, offset_by):
        used = int((tallies > 0).sum())
        fixed = max(1, used // 4)
        passed = fixed + (places - fixed + offset_by * (used - fixed)) % max(1, amount - fixed)
        return jnp.zeros((amount,), jnp.int32).at[ranking[jnp.where(places < fixed, places, passed)]].set(jnp.asarray(tallies, jnp.int32))

    tallies = jnp.where(number % 4 == 0, named(heavy_load, number // 4), named(ordinary, number - number // 4 - 1))
    mixed = jax.random.permutation(jax.random.fold_in(own, 3), amount)
    donor, sink = mixed[0:amount // 2 * 2:2], mixed[1:amount // 2 * 2:2]
    slack = jnp.minimum(tallies[donor] - 1, most - tallies[sink]) // 2
    slack = jnp.where((donor == ranking[0]) | (sink == ranking[0]) | (tallies[sink] == 0), 0, jnp.maximum(slack, 0))
    passed = jax.random.randint(jax.random.fold_in(own, 4), (amount // 2,), 0, 1 << 20) % (slack + 1)
    tallies = tallies.at[donor].add(-passed).at[sink].add(passed)
    members = jnp.searchsorted(jnp.cumsum(tallies), jnp.arange(rows * top), side="right").astype(jnp.int32)
    grid = members.reshape(top, rows).T
    grid = grid[jax.random.permutation(jax.random.fold_in(own, 1), rows)]
    offset_by = jax.random.randint(jax.random.fold_in(own, 2), (rows, 1), 0, top)
    return jnp.take_along_axis(grid, (jnp.arange(top)[None, :] + offset_by) % top, axis=1)


def load_shares(amount, total, reach, slope, full):
    loads = [(1 << 20) // math.isqrt(standing ** slope) + 1 for standing in range(1, amount + 1)]
    largest = reach if full else min(reach, max(-(-total // amount), total * loads[0] // sum(loads)))
    least = 1 if total - largest >= amount - 1 else 0
    counts, spare = [largest] + [least] * (amount - 1), total - largest - least * (amount - 1)
    while spare > 0:
        free = [i for i in range(1, amount) if counts[i] < largest] or [i for i in range(1, amount) if counts[i] < reach]
        mass, left = sum([loads[i] for i in free]), spare
        for i in free:
            addition = min(reach - counts[i], max(1, left * loads[i] // mass), spare)
            counts[i] = counts[i] + addition
            spare = spare - addition
    return np.array(counts)


def noise(own_key, shape, deviation, bound, pieces=(), kind=jnp.bfloat16):
    result = jax.random.normal(own_key, shape, jnp.float32) * deviation
    if len(pieces) > 0:
        result = block_levels(own_key, shape, pieces, -0.22, 0.18) * result
    return jnp.clip(result, min=-bound, max=bound).astype(kind)


def setup_inputs(seed: int = 0) -> dict:
    seeds = jax.random.split(jax.random.key(seed), 9)
    queries = draw_queries(jax.random.fold_in(seeds[8], 71), 0)
    key_states = draw_key_states(jax.random.fold_in(seeds[8], 71), 0)
    value_states = noise(seeds[2], (TOKENS, KVH, HD), 1.0, 6.0, ((0, 32),))
    outputs = noise(seeds[3], (TOKENS, QH, HD), 1.0, 6.0, ((0, 32),))
    output_grad = noise(seeds[4], (TOKENS, QH, HD), 16.0, 96.0, ((0, 32),))
    logsumexp = jnp.clip(6.8 + 1.0 * jax.random.uniform(seeds[5], (TOKENS, QH), jnp.float32) ** block_levels(seeds[5], (TOKENS, QH), ((0, 32),), -0.2, 0.2), 6.8, 7.8)
    random_owner_keys = jax.random.split(jax.random.fold_in(seeds[6], 1), NB // QB)
    random_owner_turns = jax.random.permutation(jax.random.fold_in(seeds[6], 3), NB // QB)
    random_owner = jax.vmap(lambda own, number: shared_out(jax.random.fold_in(seeds[6], 2), own, number, QB, N_SEQ, RND, MOST, 2))(random_owner_keys, random_owner_turns).reshape((NB, RND))
    random_slot = set_ends(jax.random.randint(seeds[7], (NB, RND), 0, QB), jax.random.fold_in(seeds[7], 1), 0, QB - 1).astype(jnp.int32)
    return dict(queries=queries, key_states=key_states, value_states=value_states, outputs=outputs, output_grad=output_grad, logsumexp=logsumexp, random_owner=random_owner, random_slot=random_slot)


def narrow_value(values):
    return lax.optimization_barrier(values.astype(jnp.bfloat16)).astype(values.dtype)


def block_lists(block_id, random_owner, random_slot):
    global_ids = jnp.arange(G, dtype=jnp.int32)
    window_ids = block_id + jnp.arange(-1, 2, dtype=jnp.int32)
    random_ids = (random_owner[block_id] * QB + random_slot[block_id]).astype(jnp.int32)
    window_ok = (window_ids >= G) & (window_ids <= NB - 1)
    random_ok = (random_ids >= G) & (jnp.abs(random_ids - block_id) >= 2)
    validity = jnp.concatenate([jnp.ones((G,), jnp.float32), window_ok.astype(jnp.float32), random_ok.astype(jnp.float32)])
    indices = jnp.clip(jnp.concatenate([global_ids, window_ids, random_ids]), 0, NB - 1).astype(jnp.int32)
    return indices, validity


def block_grads(query_block, grad_block, logsum_block, delta_block, key_blocks, value_blocks, validity):
    scaling = 1.0 / (HD ** 0.5)
    scores = jnp.einsum("ighd,mjgd->mghij", query_block, key_blocks) * scaling
    weights = jnp.exp(scores - jnp.transpose(logsum_block, (1, 2, 0))[None, :, :, :, None]) * validity[:, None, None, None, None]
    weights_rounded = narrow_value(weights)
    weight_grad = jnp.einsum("ighd,mjgd->mghij", grad_block, value_blocks)
    score_grad = narrow_value(weights * (weight_grad - jnp.transpose(delta_block, (1, 2, 0))[None, :, :, :, None]))
    query_part = jnp.einsum("mghij,mjgd->ighd", score_grad, key_blocks) * scaling
    key_part = jnp.einsum("mghij,ighd->mjgd", score_grad, query_block) * scaling
    value_part = jnp.einsum("mghij,ighd->mjgd", weights_rounded, grad_block)
    return query_part, jnp.stack([key_part, value_part], axis=2)


def reference(queries, key_states, value_states, outputs, output_grad, logsumexp, random_owner, random_slot):
    group = QH // KVH
    query_full = queries.astype(jnp.float32).reshape(NB, BLK, KVH, group, HD)
    grad_full = output_grad.astype(jnp.float32).reshape(NB, BLK, KVH, group, HD)
    row_delta = jnp.sum(output_grad.astype(jnp.float32) * outputs.astype(jnp.float32), axis=-1)
    delta_blocks = row_delta.reshape(NB, BLK, KVH, group)
    logsum_blocks = logsumexp.reshape(NB, BLK, KVH, group)
    kv_blocks = jnp.stack([key_states, value_states], axis=1).astype(jnp.float32).reshape(NB, BLK, 2, KVH, HD)

    def advance(carry, block_id):
        indices, validity = block_lists(block_id, random_owner, random_slot)
        chosen = kv_blocks[indices]
        query_part, kv_part = block_grads(query_full[block_id], grad_full[block_id], logsum_blocks[block_id], delta_blocks[block_id], chosen[:, :, 0], chosen[:, :, 1], validity)
        carry = carry.at[indices].add(kv_part)
        return carry, query_part

    initial = jnp.zeros((NB, BLK, 2, KVH, HD), jnp.float32)
    kv_grad, query_parts = lax.scan(advance, initial, jnp.arange(NB, dtype=jnp.int32))
    query_grad = query_parts.reshape(TOKENS, QH, HD).astype(jnp.bfloat16)
    key_grad = kv_grad[:, :, 0].reshape(TOKENS, KVH, HD).astype(jnp.bfloat16)
    value_grad = kv_grad[:, :, 1].reshape(TOKENS, KVH, HD).astype(jnp.bfloat16)
    return (query_grad, key_grad, value_grad)
```

```python
import functools
import math

import jax
import jax.numpy as jnp
from jax import lax
from jax.experimental import pallas as pl
from jax.experimental.pallas import tpu as pltpu
from jax.sharding import PartitionSpec as P

HD = 128
BLK = 128
G = 2
RND = 3
MESH = pl.DeviceIdType.MESH
F32 = jnp.float32
BF16 = jnp.bfloat16
LOG2E = math.log2(math.e)


def greet(n_seq, n_head, seq, head):
    barrier = pltpu.get_barrier_semaphore()

    def to_head(d, c):
        pl.semaphore_signal(
            barrier, inc=1, device_id={"head": lax.rem(head + d, n_head)}, device_id_type=MESH
        )
        return c

    def to_seq(d, c):
        pl.semaphore_signal(
            barrier, inc=1, device_id={"seq": lax.rem(seq + d, n_seq)}, device_id_type=MESH
        )
        return c

    lax.fori_loop(1, n_head, to_head, 0)
    lax.fori_loop(1, n_seq, to_seq, 0)
    pl.semaphore_wait(barrier, n_head + n_seq - 2)


def remote(src, dst, send, recv, **where):
    return pltpu.make_async_remote_copy(
        src_ref=src,
        dst_ref=dst,
        send_sem=send,
        recv_sem=recv,
        device_id=where,
        device_id_type=MESH,
    )


def exchange_in(
    n_seq, n_head, most,
    pick, q_in, g_in, kv_in, ld_in,
    q_out, g_out, ld_out, kv_out, glob_out, rand_out,
    picked, held, hs, hr, ls, ss, sr, ns, nr, gs, gr,
):
    seq, head = lax.axis_index("seq"), lax.axis_index("head")
    rows = q_in.shape[1]
    toks = kv_in.shape[2]
    span = n_head * toks
    greet(n_seq, n_head, seq, head)

    q_to = q_out.at[pl.ds(pl.multiple_of(head * rows, rows), rows), :]
    g_to = g_out.at[pl.ds(pl.multiple_of(head * rows, rows), rows), :]
    kv_to = kv_out.at[:, pl.ds(pl.multiple_of(BLK + head * toks, 32), toks), :]
    ld_to = ld_out.at[head]

    def head_copy(kind, d):
        peer = lax.rem(head + d, n_head)
        src, dst = (
            (kv_in.at[peer], kv_to),
            (ld_in.at[peer], ld_to),
            (q_in.at[peer], q_to),
            (g_in.at[peer], g_to),
        )[kind]
        return remote(src, dst, hs.at[kind, d], hr.at[kind, d], head=peer)

    own = [
        pltpu.make_async_copy(kv_in.at[head], kv_to, ls.at[0]),
        pltpu.make_async_copy(ld_in.at[head], ld_to, ls.at[1]),
        pltpu.make_async_copy(q_in.at[head], q_to, ls.at[2]),
        pltpu.make_async_copy(g_in.at[head], g_to, ls.at[3]),
    ]
    for kind in range(4):
        for d in range(1, n_head):
            head_copy(kind, d).start()
        own[kind].start()
    own[0].wait()
    for d in range(1, n_head):
        head_copy(0, d).wait_recv()

    up, down = lax.rem(seq + 1, n_seq), lax.rem(seq + n_seq - 1, n_seq)
    to_up = remote(
        kv_out.at[:, pl.ds(span, BLK), :], kv_out.at[:, pl.ds(0, BLK), :],
        ns.at[0], nr.at[0], seq=up,
    )
    to_down = remote(
        kv_out.at[:, pl.ds(BLK, BLK), :], kv_out.at[:, pl.ds(BLK + span, BLK), :],
        ns.at[1], nr.at[1], seq=down,
    )

    def rand_copy(d):
        peer = lax.rem(seq + d, n_seq)
        return remote(picked.at[peer], rand_out.at[seq], ss.at[d], sr.at[d], seq=peer)

    def glob_copy(d):
        return remote(
            kv_out.at[:, pl.ds(BLK, G * BLK), :], glob_out, gs.at[d], gr, seq=d
        )

    def fill(d, c):
        peer = lax.rem(seq + d, n_seq)
        for m in range(most):
            picked[peer, m] = held[pick[peer * most + m]]
        return c

    def start(d, c):
        rand_copy(d).start()
        return c

    def finish(d, c):
        rand_copy(d).wait()
        return c

    for block in range(span // BLK):
        held[block] = kv_out[:, (block + 1) * BLK : (block + 2) * BLK, :]
    lax.fori_loop(0, n_seq, fill, 0)
    to_up.start()
    to_down.start()

    @pl.when(seq == 0)
    def _():
        def go(d, c):
            glob_copy(d).start()
            return c

        lax.fori_loop(1, n_seq, go, 0)
        glob_out[...] = kv_out[:, BLK : BLK + G * BLK, :]

    lax.fori_loop(1, n_seq, start, 0)
    rand_out[seq] = picked[seq]
    for kind in range(1, 4):
        own[kind].wait()
        for d in range(1, n_head):
            head_copy(kind, d).wait_recv()
    for kind in range(4):
        for d in range(1, n_head):
            head_copy(kind, d).wait_send()
    to_up.wait()
    to_down.wait()

    @pl.when(seq == 0)
    def _():
        def done(d, c):
            glob_copy(d).wait_send()
            return c

        lax.fori_loop(1, n_seq, done, 0)

    @pl.when(seq > 0)
    def _():
        glob_copy(0).wait_recv()

    lax.fori_loop(1, n_seq, finish, 0)


def dot(a, b, ca, cb):
    return lax.dot_general(a, b, (((ca,), (cb,)), ((), ())), preferred_element_type=F32)


def attend(
    blocks, pos, bias,
    q_ref, g_ref, ld_ref, kv_ref, glob_ref, rand_ref,
    dq_ref, own_ref, halo_ref, gpart_ref, rpart_ref,
    kcat, vcat, acc, gacc,
):
    b = pl.program_id(0)
    scaling = 1.0 / HD**0.5

    @pl.when(b == 0)
    def _():
        acc[...] = jnp.zeros_like(acc)
        gacc[...] = jnp.zeros_like(gacc)
        rpart_ref[...] = jnp.zeros_like(rpart_ref)

    at = pl.multiple_of(b * BLK, BLK)
    win = pl.ds(at, 3 * BLK)
    first = G * BLK
    last = first + 3 * BLK
    kcat[0:first] = glob_ref[0]
    vcat[0:first] = glob_ref[1]
    kcat[first:last] = kv_ref[0, win, :]
    vcat[first:last] = kv_ref[1, win, :]
    for j in range(RND):
        spot = pos[b * RND + j]
        kcat[last + j * BLK : last + (j + 1) * BLK] = rand_ref[spot, 0]
        vcat[last + j * BLK : last + (j + 1) * BLK] = rand_ref[spot, 1]

    q = q_ref[...]
    g = g_ref[...]
    count = ld_ref.shape[1]
    lse = jnp.concatenate([ld_ref[0, r : r + 1, :] for r in range(count)], axis=1) * LOG2E
    delta = jnp.concatenate([ld_ref[1, r : r + 1, :] for r in range(count)], axis=1)
    dq = None
    for pair in range((G + 3 + RND) // 2):
        span = pl.ds(pair * 2 * BLK, 2 * BLK)
        k = kcat[span, :]
        v = vcat[span, :]
        scores = dot(k, q, 1, 1) * (scaling * LOG2E)
        grads = dot(v, g, 1, 1) - delta
        halves = []
        for half in range(2):
            which = pair * 2 + half
            shift = lse
            if which >= G:
                shift = lse + bias[b * (3 + RND) + which - G]
            halves.append(jnp.exp2(scores[half * BLK : (half + 1) * BLK] - shift))
        weights = jnp.concatenate(halves, axis=0)
        score_grad = (weights * grads).astype(BF16)
        dv = dot(weights.astype(BF16), g, 1, 0)
        dk = dot(score_grad, q, 1, 0) * scaling
        part = dot(k, score_grad, 0, 0)
        dq = part if dq is None else dq + part
        for half in range(2):
            which = pair * 2 + half
            dk_half = dk[half * BLK : (half + 1) * BLK]
            dv_half = dv[half * BLK : (half + 1) * BLK]
            if which < G:
                gacc[0, which * BLK : (which + 1) * BLK, :] += dk_half
                gacc[1, which * BLK : (which + 1) * BLK, :] += dv_half
            elif which < G + 3:
                rows = pl.ds(pl.multiple_of(at + (which - G) * BLK, BLK), BLK)
                acc[0, rows, :] += dk_half
                acc[1, rows, :] += dv_half
            else:
                spot = pos[b * RND + which - G - 3]
                rpart_ref[spot, 0] = dk_half.astype(BF16)
                rpart_ref[spot, 1] = dv_half.astype(BF16)
    dq_ref[...] = (dq.T * scaling).astype(BF16)

    @pl.when(b == blocks - 1)
    def _():
        own_ref[...] = acc[:, BLK : BLK + blocks * BLK, :]
        halo_ref[0] = acc[:, 0:BLK, :].astype(BF16)
        halo_ref[1] = acc[:, BLK + blocks * BLK :, :].astype(BF16)
        gpart_ref[...] = gacc[...].astype(BF16)


def exchange_out(
    n_seq, n_head, most,
    share, dq_in, own_in, halo_in, gpart_in, rpart_in,
    dq_out, kv_out,
    halo, gall, rback, kv_sum, hs, hr, ls, ss, sr, ns, nr, gs, gr,
):
    seq, head = lax.axis_index("seq"), lax.axis_index("head")
    rows = dq_out.shape[1]
    toks = kv_out.shape[2]
    blocks = own_in.shape[1] // BLK
    greet(n_seq, n_head, seq, head)

    def rand_copy(d):
        peer = lax.rem(seq + d, n_seq)
        return remote(rpart_in.at[peer], rback.at[seq], ss.at[d], sr.at[d], seq=peer)

    def glob_copy():
        return remote(gpart_in, gall.at[seq], gs, gr.at[seq], seq=0)

    def dq_copy(d):
        peer = lax.rem(head + d, n_head)
        src = dq_in.at[pl.ds(pl.multiple_of(peer * rows, rows), rows), :]
        return remote(src, dq_out.at[head], hs.at[0, d], hr.at[0, d], head=peer)

    def kv_copy(d):
        peer = lax.rem(head + d, n_head)
        src = kv_sum.at[:, pl.ds(pl.multiple_of(peer * toks, 32), toks), :]
        return remote(src, kv_out.at[head], hs.at[1, d], hr.at[1, d], head=peer)

    up, down = lax.rem(seq + 1, n_seq), lax.rem(seq + n_seq - 1, n_seq)
    to_down = remote(halo_in.at[0], halo.at[0], ns.at[0], nr.at[0], seq=down)
    to_up = remote(halo_in.at[1], halo.at[1], ns.at[1], nr.at[1], seq=up)
    own_dq = pltpu.make_async_copy(
        dq_in.at[pl.ds(pl.multiple_of(head * rows, rows), rows), :], dq_out.at[head], ls.at[0]
    )

    to_down.start()
    to_up.start()

    @pl.when(seq > 0)
    def _():
        glob_copy().start()

    def start(d, c):
        rand_copy(d).start()
        return c

    lax.fori_loop(1, n_seq, start, 0)
    for d in range(1, n_head):
        dq_copy(d).start()
    own_dq.start()

    rback[seq] = rpart_in[seq]
    to_down.wait()
    to_up.wait()

    @pl.when(seq > 0)
    def _():
        gall[0] = jnp.zeros(gall.shape[1:], BF16)
        glob_copy().wait_send()

    @pl.when(seq == 0)
    def _():
        gall[0] = gpart_in[...]

        def arrive(d, c):
            remote(gpart_in, gall.at[d], gs, gr.at[d], seq=0).wait_recv()
            return c

        lax.fori_loop(1, n_seq, arrive, 0)

    @pl.when(seq > 0)
    def _():
        def blank(d, c):
            gall[d] = jnp.zeros(gall.shape[1:], BF16)
            return c

        lax.fori_loop(1, n_seq, blank, 0)

    def finish(d, c):
        rand_copy(d).wait()
        return c

    lax.fori_loop(1, n_seq, finish, 0)

    def gather(block, c):
        spot = pl.ds(pl.multiple_of(block * BLK, BLK), BLK)
        for part in range(2):

            def add(p, total):
                for m in range(most):
                    total = total + share[block, p * most + m] * rback[p, m, part].astype(F32)
                return total

            total = lax.fori_loop(0, n_seq, add, own_in[part, spot, :])
            kv_sum[part, spot, :] = total.astype(BF16)
        return c

    def edge(block, extra):
        spot = pl.ds(block * BLK, BLK)
        for part in range(2):

            def add(p, total):
                for m in range(most):
                    total = total + share[block, p * most + m] * rback[p, m, part].astype(F32)
                return total

            total = own_in[part, spot, :]
            for term in extra(part):
                total = total + term
            total = lax.fori_loop(0, n_seq, add, total)
            kv_sum[part, spot, :] = total.astype(BF16)

    def glob_term(part, block):
        def add(p, total):
            return total + gall[p, part, block * BLK : (block + 1) * BLK, :].astype(F32)

        return lax.fori_loop(0, n_seq, add, jnp.zeros((BLK, HD), F32))

    for block in range(blocks):
        if block < G or block == blocks - 1:

            def extra(part, block=block):
                terms = []
                if block == 0:
                    terms.append(halo[1, part].astype(F32))
                if block == blocks - 1:
                    terms.append(halo[0, part].astype(F32))
                if block < G:
                    terms.append(glob_term(part, block))
                return terms

            edge(block, extra)
    lax.fori_loop(G, blocks - 1, gather, 0)

    own_kv = pltpu.make_async_copy(
        kv_sum.at[:, pl.ds(pl.multiple_of(head * toks, 32), toks), :], kv_out.at[head], ls.at[1]
    )
    for d in range(1, n_head):
        kv_copy(d).start()
    own_kv.start()
    own_dq.wait()
    for d in range(1, n_head):
        dq_copy(d).wait()
    own_kv.wait()
    for d in range(1, n_head):
        kv_copy(d).wait()


def per_device(
    n_seq, n_head,
    queries, key_states, value_states, outputs, output_grad, logsumexp, random_owner, random_slot,
):
    toks, heads, _ = queries.shape
    group = heads // n_head
    rows = toks * group
    span = toks * n_head
    blocks = span // BLK
    per_row = blocks * RND
    most = max(1, (per_row + n_seq - 1) // n_seq)
    seq = lax.axis_index("seq")
    vmem = pl.BlockSpec(memory_space=pltpu.VMEM)
    smem = pl.BlockSpec(memory_space=pltpu.SMEM)
    hbm = pl.BlockSpec(memory_space=pl.ANY)
    dma = pltpu.SemaphoreType.DMA

    delta = jnp.sum(output_grad.astype(F32) * outputs.astype(F32), axis=-1)

    def by_head(x):
        return jnp.transpose(x.reshape(toks, n_head, group, HD), (1, 0, 2, 3)).reshape(
            n_head, rows, HD
        )

    ld = jnp.stack([logsumexp, delta]).reshape(2, toks, n_head, group)
    ld = jnp.transpose(ld, (2, 0, 1, 3)).reshape(n_head, 2, rows // 128, 128)
    kv = jnp.transpose(jnp.stack([key_states, value_states]), (2, 0, 1, 3))

    owner_table = random_owner.reshape(n_seq, per_row)
    slot_table = random_slot.reshape(n_seq, per_row)
    entry = jnp.arange(per_row, dtype=jnp.int32)
    rank_table = jnp.sum(
        (
            (owner_table[:, :, None] == owner_table[:, None, :])
            & (entry[None, :] < entry[:, None])[None]
        ).astype(jnp.int32),
        axis=2,
    )
    hits = (owner_table == seq)[:, :, None] & (
        rank_table[:, :, None] == jnp.arange(most, dtype=jnp.int32)
    )
    pick = jnp.sum(jnp.where(hits, slot_table[:, :, None] + 1, 0), axis=1).reshape(-1) - 1
    share = (pick[None, :] == jnp.arange(blocks, dtype=jnp.int32)[:, None]).astype(F32)
    my_owner = lax.dynamic_slice_in_dim(owner_table, seq, 1, 0).reshape(-1)
    my_slot = lax.dynamic_slice_in_dim(slot_table, seq, 1, 0).reshape(-1)
    my_rank = lax.dynamic_slice_in_dim(rank_table, seq, 1, 0).reshape(-1)
    pos = my_owner * most + my_rank
    ids = seq * blocks + jnp.arange(blocks, dtype=jnp.int32)
    near = ids[:, None] + jnp.arange(-1, 2, dtype=jnp.int32)[None, :]
    far = (my_owner * blocks + my_slot).reshape(blocks, RND)
    okay = jnp.concatenate(
        [
            (near >= G) & (near <= n_seq * blocks - 1),
            (far >= G) & (jnp.abs(far - ids[:, None]) >= 2),
        ],
        axis=1,
    )
    bias = jnp.where(okay, 0.0, 1e30).astype(F32).reshape(-1)

    q_loc, g_loc, ld_loc, kv_ext, glob, fetched = pl.pallas_call(
        functools.partial(exchange_in, n_seq, n_head, most),
        out_shape=[
            jax.ShapeDtypeStruct((n_head * rows, HD), BF16),
            jax.ShapeDtypeStruct((n_head * rows, HD), BF16),
            jax.ShapeDtypeStruct((n_head, 2, rows // 128, 128), F32),
            jax.ShapeDtypeStruct((2, span + 2 * BLK, HD), BF16),
            jax.ShapeDtypeStruct((2, G * BLK, HD), BF16),
            jax.ShapeDtypeStruct((n_seq, most, 2, BLK, HD), BF16),
        ],
        in_specs=[smem, hbm, hbm, vmem, vmem],
        out_specs=[vmem] * 6,
        scratch_shapes=[
            pltpu.VMEM((n_seq, most, 2, BLK, HD), BF16),
            pltpu.VMEM((blocks, 2, BLK, HD), BF16),
            dma((4, n_head)), dma((4, n_head)), dma((4,)),
            dma((n_seq,)), dma((n_seq,)), dma((2,)), dma((2,)), dma((n_seq,)), dma,
        ],
        compiler_params=pltpu.CompilerParams(
            collective_id=0, has_side_effects=True, vmem_limit_bytes=56 << 20
        ),
        name="exchange_in",
    )(jnp.maximum(pick, 0), by_head(queries), by_head(output_grad), kv, ld)

    ld_all = jnp.transpose(ld_loc, (1, 0, 2, 3)).reshape(2, n_head * rows // 128, 128)
    fetched = fetched.reshape(n_seq * most, 2, BLK, HD)
    step = BLK * group
    dq, own, halo, gpart, rpart = pl.pallas_call(
        functools.partial(attend, blocks),
        grid=(blocks,),
        out_shape=[
            jax.ShapeDtypeStruct((n_head * rows, HD), BF16),
            jax.ShapeDtypeStruct((2, span, HD), F32),
            jax.ShapeDtypeStruct((2, 2, BLK, HD), BF16),
            jax.ShapeDtypeStruct((2, G * BLK, HD), BF16),
            jax.ShapeDtypeStruct((n_seq * most, 2, BLK, HD), BF16),
        ],
        in_specs=[
            smem,
            smem,
            pl.BlockSpec((step, HD), lambda b: (b, 0)),
            pl.BlockSpec((step, HD), lambda b: (b, 0)),
            pl.BlockSpec((2, step // 128, 128), lambda b: (0, b, 0)),
            vmem, vmem, vmem,
        ],
        out_specs=[pl.BlockSpec((step, HD), lambda b: (b, 0)), vmem, vmem, vmem, vmem],
        scratch_shapes=[
            pltpu.VMEM(((G + 3 + RND) * BLK, HD), BF16),
            pltpu.VMEM(((G + 3 + RND) * BLK, HD), BF16),
            pltpu.VMEM((2, span + 2 * BLK, HD), F32),
            pltpu.VMEM((2, G * BLK, HD), F32),
        ],
        compiler_params=pltpu.CompilerParams(
            dimension_semantics=("arbitrary",), vmem_limit_bytes=56 << 20
        ),
        name="attend",
    )(pos, bias, q_loc, g_loc, ld_all, kv_ext, glob, fetched)

    dq_all, kv_all = pl.pallas_call(
        functools.partial(exchange_out, n_seq, n_head, most),
        out_shape=[
            jax.ShapeDtypeStruct((n_head, rows, HD), BF16),
            jax.ShapeDtypeStruct((n_head, 2, toks, HD), BF16),
        ],
        in_specs=[smem] + [vmem] * 5,
        out_specs=[vmem, vmem],
        scratch_shapes=[
            pltpu.VMEM((2, 2, BLK, HD), BF16),
            pltpu.VMEM((n_seq, 2, G * BLK, HD), BF16),
            pltpu.VMEM((n_seq, most, 2, BLK, HD), BF16),
            pltpu.VMEM((2, span, HD), BF16),
            dma((2, n_head)), dma((2, n_head)), dma((2,)),
            dma((n_seq,)), dma((n_seq,)), dma((2,)), dma((2,)), dma, dma((n_seq,)),
        ],
        compiler_params=pltpu.CompilerParams(
            collective_id=1, has_side_effects=True, vmem_limit_bytes=56 << 20
        ),
        name="exchange_out",
    )(share, dq, own, halo, gpart, rpart.reshape(n_seq, most, 2, BLK, HD))

    query_grad = jnp.transpose(
        dq_all.reshape(n_head, toks, group, HD), (1, 0, 2, 3)
    ).reshape(toks, heads, HD)
    key_grad = jnp.transpose(kv_all[:, 0], (1, 0, 2))
    value_grad = jnp.transpose(kv_all[:, 1], (1, 0, 2))
    return query_grad, key_grad, value_grad


def solution(mesh):
    wide = P(("seq", "head"), None, None)
    return jax.shard_map(
        functools.partial(per_device, mesh.shape["seq"], mesh.shape["head"]),
        mesh=mesh,
        in_specs=(wide, wide, wide, wide, wide, P(("seq", "head"), None), P(), P()),
        out_specs=(wide, wide, wide),
        check_vma=False,
    )
```

```python
import functools
import math

import jax
import jax.numpy as jnp
from jax import lax
from jax.experimental import pallas as pl
from jax.experimental.pallas import tpu as pltpu
from jax.sharding import PartitionSpec as P

HD = 128
BLK = 128
G = 2
RND = 3
MESH = pl.DeviceIdType.MESH
F32 = jnp.float32
BF16 = jnp.bfloat16
LOG2E = math.log2(math.e)


def greet(n_seq, n_head, seq, head):
    barrier = pltpu.get_barrier_semaphore()

    def to_head(d, c):
        pl.semaphore_signal(
            barrier, inc=1, device_id={"head": lax.rem(head + d, n_head)}, device_id_type=MESH
        )
        return c

    def to_seq(d, c):
        pl.semaphore_signal(
            barrier, inc=1, device_id={"seq": lax.rem(seq + d, n_seq)}, device_id_type=MESH
        )
        return c

    lax.fori_loop(1, n_head, to_head, 0)
    lax.fori_loop(1, n_seq, to_seq, 0)
    pl.semaphore_wait(barrier, n_head + n_seq - 2)


def remote(src, dst, send, recv, **where):
    return pltpu.make_async_remote_copy(
        src_ref=src,
        dst_ref=dst,
        send_sem=send,
        recv_sem=recv,
        device_id=where,
        device_id_type=MESH,
    )


def dot(a, b, ca, cb):
    return lax.dot_general(a, b, (((ca,), (cb,)), ((), ())), preferred_element_type=F32)


def pair_grads(k, v, shifts, q, g, delta, scaling):
    scores = dot(k, q, 1, 1) * (scaling * LOG2E)
    weights = jnp.concatenate(
        [jnp.exp2(scores[i * BLK : (i + 1) * BLK] - shift) for i, shift in enumerate(shifts)],
        axis=0,
    )
    score_grad = (weights * (dot(v, g, 1, 1) - delta)).astype(BF16)
    dv = dot(weights.astype(BF16), g, 1, 0)
    dk = dot(score_grad, q, 1, 0) * scaling
    return dk, dv, dot(k, score_grad, 0, 0)


def fused(
    n_seq, n_head, most, blocks,
    pick, pos, back, bias, share, q_in, g_in, kv_in, ld_in,
    dq_out, kv_out,
    q_all, g_all, ld_all, kv_ext, glob, rand, picked, held, acc, gacc, dq_acc, dq_all,
    rpart, rback, halo_part, halo, gpart, gall, kv_sum,
    hs, hr, ls, ss, sr, ns, nr, gs, gr, rs, rr,
):
    seq, head = lax.axis_index("seq"), lax.axis_index("head")
    rows = q_in.shape[1]
    toks = kv_in.shape[2]
    span = n_head * toks
    lines = rows // 128
    step = rows * n_head // blocks
    scaling = 1.0 / HD**0.5
    greet(n_seq, n_head, seq, head)

    def partner(d):
        base = lax.rem(head + 2 * (d // 2), n_head)
        return base + (1 - 2 * lax.rem(base, 2)) if d % 2 else base

    mine = pl.ds(pl.multiple_of(head * rows, rows), rows)
    q_to = q_all.at[mine, :]
    g_to = g_all.at[mine, :]
    kv_to = kv_ext.at[:, pl.ds(pl.multiple_of(BLK + head * toks, 32), toks), :]
    ld_to = ld_all.at[:, pl.ds(head * lines, lines)]

    def head_copy(kind, d):
        peer = partner(d)
        src, dst = (
            (kv_in.at[peer], kv_to),
            (ld_in.at[peer], ld_to),
            (q_in.at[peer], q_to),
            (g_in.at[peer], g_to),
        )[kind]
        return remote(src, dst, hs.at[kind, d], hr.at[kind, d], head=peer)

    own = [
        pltpu.make_async_copy(kv_in.at[head], kv_to, ls.at[0]),
        pltpu.make_async_copy(ld_in.at[head], ld_to, ls.at[1]),
        pltpu.make_async_copy(q_in.at[head], q_to, ls.at[2]),
        pltpu.make_async_copy(g_in.at[head], g_to, ls.at[3]),
    ]
    for kind in range(4):
        own[kind].start()
    for kind in range(4):
        for d in list(range(2, n_head)) + [1]:
            head_copy(kind, d).start()
    own[0].wait()
    for d in range(1, n_head):
        head_copy(0, d).wait_recv()

    up, down = lax.rem(seq + 1, n_seq), lax.rem(seq + n_seq - 1, n_seq)
    to_up = remote(
        kv_ext.at[:, pl.ds(span, BLK), :], kv_ext.at[:, pl.ds(0, BLK), :],
        ns.at[0], nr.at[0], seq=up,
    )
    to_down = remote(
        kv_ext.at[:, pl.ds(BLK, BLK), :], kv_ext.at[:, pl.ds(BLK + span, BLK), :],
        ns.at[1], nr.at[1], seq=down,
    )

    def rand_copy(d):
        peer = lax.rem(seq + d, n_seq)
        return remote(
            picked.at[pl.ds(peer * most, most)], rand.at[pl.ds(seq * most, most)],
            ss.at[d], sr.at[d], seq=peer,
        )

    def glob_copy(d):
        return remote(kv_ext.at[:, pl.ds(BLK, G * BLK), :], glob, gs.at[d], gr.at[0], seq=d)

    def loop(low, high, body):
        def run(i, c):
            body(i)
            return c

        lax.fori_loop(low, high, run, 0)

    def fill(i):
        picked[i] = held[pick[i]]

    for block in range(blocks):
        held[block] = kv_ext[:, (block + 1) * BLK : (block + 2) * BLK, :]
    loop(0, n_seq * most, fill)
    to_up.start()
    to_down.start()

    @pl.when(seq == 0)
    def _():
        loop(1, n_seq, lambda d: glob_copy(d).start())
        glob[...] = kv_ext[:, BLK : BLK + G * BLK, :]

    loop(1, n_seq, lambda d: rand_copy(d).start())
    rand[pl.ds(seq * most, most)] = picked[pl.ds(seq * most, most)]

    acc[...] = jnp.zeros_like(acc)
    gacc[...] = jnp.zeros_like(gacc)
    to_up.wait()
    to_down.wait()

    @pl.when(seq > 0)
    def _():
        glob_copy(0).wait_recv()

    for kind in range(1, 4):
        own[kind].wait()
        head_copy(kind, 1).wait_recv()
    for d in range(2, n_head):
        head_copy(1, d).wait_recv()

    turn = head // (n_head // 2)

    def order(i):
        return i + turn * (blocks - 1 - 2 * i)

    def operands(b):
        spot = pl.ds(pl.multiple_of(b * step, step), step)
        per = step // 128

        def lanes(part):
            tile = ld_all[part, pl.ds(b * per, per)]
            return jnp.concatenate([tile[r] for r in range(per)], axis=1)

        return q_all[spot, :], g_all[spot, :], lanes(0) * LOG2E, lanes(1)

    def near(i, fresh):
        b = order(i)
        q, g, lse, delta = operands(b)
        at = pl.multiple_of(b * BLK, BLK)
        win = pl.ds(at, 3 * BLK)
        dk, dv, dq = pair_grads(glob[0], glob[1], [lse] * G, q, g, delta, scaling)
        gacc[0] += dk
        gacc[1] += dv
        shifts = [lse + bias[b * (3 + RND) + j] for j in range(3)]
        dk, dv, more = pair_grads(kv_ext[0, win, :], kv_ext[1, win, :], shifts, q, g, delta, scaling)
        acc[0, win, :] += dk
        acc[1, win, :] += dv
        if fresh:
            dq_acc[b] = dq + more
        else:
            total = dq_acc[b] + dq + more
            dq_all[pl.ds(pl.multiple_of(b * step, step), step), :] = (total.T * scaling).astype(BF16)

    def far(i, fresh):
        b = order(i)
        q, g, lse, delta = operands(b)
        found = [rand[pos[b * RND + j]] for j in range(RND)]
        k = jnp.concatenate([f[0] for f in found], axis=0)
        v = jnp.concatenate([f[1] for f in found], axis=0)
        shifts = [lse + bias[b * (3 + RND) + 3 + j] for j in range(RND)]
        dk, dv, dq = pair_grads(k, v, shifts, q, g, delta, scaling)
        for j in range(RND):
            rpart[b * RND + j, 0] = dk[j * BLK : (j + 1) * BLK].astype(BF16)
            rpart[b * RND + j, 1] = dv[j * BLK : (j + 1) * BLK].astype(BF16)
        if fresh:
            dq_acc[b] = dq
        else:
            total = dq_acc[b] + dq
            dq_all[pl.ds(pl.multiple_of(b * step, step), step), :] = (total.T * scaling).astype(BF16)

    early = span // 2 // BLK
    loop(0, early, lambda i: near(i, True))
    loop(1, n_seq, lambda d: rand_copy(d).wait())
    loop(0, early, lambda i: far(i, False))
    for kind in range(2, 4):
        for d in range(2, n_head):
            head_copy(kind, d).wait_recv()
    loop(early, blocks, lambda i: far(i, True))

    def gather(i):
        picked[i] = rpart[back[i]]

    def back_copy(d):
        peer = lax.rem(seq + d, n_seq)
        return remote(
            picked.at[pl.ds(peer * most, most)], rback.at[pl.ds(seq * most, most)],
            rs.at[d], rr.at[d], seq=peer,
        )

    loop(0, n_seq * most, gather)
    rback[pl.ds(seq * most, most)] = picked[pl.ds(seq * most, most)]
    loop(1, n_seq, lambda d: back_copy(d).start())
    loop(early, blocks, lambda i: near(i, False))

    halo_part[0] = acc[:, 0:BLK, :].astype(BF16)
    halo_part[1] = acc[:, BLK + span :, :].astype(BF16)
    gpart[...] = gacc[...].astype(BF16)

    def dq_copy(d):
        peer = partner(d)
        src = dq_all.at[pl.ds(pl.multiple_of(peer * rows, rows), rows), :]
        return remote(src, dq_out.at[head], hs.at[4, d], hr.at[4, d], head=peer)

    def kv_copy(d):
        peer = partner(d)
        src = kv_sum.at[:, pl.ds(pl.multiple_of(peer * toks, 32), toks), :]
        return remote(src, kv_out.at[head], hs.at[5, d], hr.at[5, d], head=peer)

    def part_copy():
        return remote(gpart, gall.at[seq], gs.at[0], gr.at[seq], seq=0)

    down_grad = remote(halo_part.at[0], halo.at[0], ns.at[2], nr.at[2], seq=down)
    up_grad = remote(halo_part.at[1], halo.at[1], ns.at[3], nr.at[3], seq=up)
    own_dq = pltpu.make_async_copy(dq_all.at[mine, :], dq_out.at[head], ls.at[4])
    for d in list(range(2, n_head)) + [1]:
        dq_copy(d).start()
    own_dq.start()
    down_grad.start()
    up_grad.start()

    @pl.when(seq > 0)
    def _():
        part_copy().start()

    for kind in range(4):
        for d in range(1, n_head):
            head_copy(kind, d).wait_send()

    @pl.when(seq == 0)
    def _():
        loop(1, n_seq, lambda d: glob_copy(d).wait_send())
        gall[0] = gpart[...]

        def arrive(d):
            remote(gpart, gall.at[d], gs.at[0], gr.at[d], seq=0).wait_recv()

        loop(1, n_seq, arrive)

        def add(d):
            gacc[...] += gall[d].astype(F32)

        loop(1, n_seq, add)
        acc[:, BLK : BLK + G * BLK, :] += gacc[...]

    @pl.when(seq > 0)
    def _():
        part_copy().wait_send()

    down_grad.wait()
    up_grad.wait()
    acc[:, BLK : 2 * BLK, :] += halo[1].astype(F32)
    acc[:, span : span + BLK, :] += halo[0].astype(F32)
    loop(1, n_seq, lambda d: back_copy(d).wait())

    def total(block):
        spot = pl.ds(pl.multiple_of(block * BLK, BLK), BLK)
        over = pl.ds(pl.multiple_of(block * BLK + BLK, BLK), BLK)
        for part in range(2):

            def add(i, value):
                return value + share[block, i] * rback[i, part].astype(F32)

            value = lax.fori_loop(0, n_seq * most, add, acc[part, over, :])
            kv_sum[part, spot, :] = value.astype(BF16)

    loop(0, blocks, total)
    own_kv = pltpu.make_async_copy(
        kv_sum.at[:, pl.ds(pl.multiple_of(head * toks, 32), toks), :], kv_out.at[head], ls.at[5]
    )
    for d in list(range(2, n_head)) + [1]:
        kv_copy(d).start()
    own_kv.start()
    own_dq.wait()
    for d in range(1, n_head):
        dq_copy(d).wait()
    own_kv.wait()
    for d in range(1, n_head):
        kv_copy(d).wait()


def per_device(
    n_seq, n_head,
    queries, key_states, value_states, outputs, output_grad, logsumexp, random_owner, random_slot,
):
    toks, heads, _ = queries.shape
    group = heads // n_head
    rows = toks * group
    span = toks * n_head
    blocks = span // BLK
    per_row = blocks * RND
    most = max(1, (per_row + n_seq - 1) // n_seq)
    seq = lax.axis_index("seq")
    vmem = pl.BlockSpec(memory_space=pltpu.VMEM)
    smem = pl.BlockSpec(memory_space=pltpu.SMEM)
    hbm = pl.BlockSpec(memory_space=pl.ANY)
    dma = pltpu.SemaphoreType.DMA

    delta = jnp.sum(output_grad.astype(F32) * outputs.astype(F32), axis=-1)

    def by_head(x):
        return jnp.transpose(x.reshape(toks, n_head, group, HD), (1, 0, 2, 3)).reshape(
            n_head, rows, HD
        )

    ld = jnp.stack([logsumexp, delta]).reshape(2, toks, n_head, group)
    ld = jnp.transpose(ld, (2, 0, 1, 3)).reshape(n_head, 2, rows // 128, 1, 128)
    kv = jnp.transpose(jnp.stack([key_states, value_states]), (2, 0, 1, 3))

    owner_table = random_owner.reshape(n_seq, per_row)
    slot_table = random_slot.reshape(n_seq, per_row)
    entry = jnp.arange(per_row, dtype=jnp.int32)
    rank_table = jnp.sum(
        (
            (owner_table[:, :, None] == owner_table[:, None, :])
            & (entry[None, :] < entry[:, None])[None]
        ).astype(jnp.int32),
        axis=2,
    )
    hits = (owner_table == seq)[:, :, None] & (
        rank_table[:, :, None] == jnp.arange(most, dtype=jnp.int32)
    )
    pick = jnp.sum(jnp.where(hits, slot_table[:, :, None] + 1, 0), axis=1).reshape(-1) - 1
    share = (pick[None, :] == jnp.arange(blocks, dtype=jnp.int32)[:, None]).astype(F32)
    my_owner = lax.dynamic_slice_in_dim(owner_table, seq, 1, 0).reshape(-1)
    my_slot = lax.dynamic_slice_in_dim(slot_table, seq, 1, 0).reshape(-1)
    my_rank = lax.dynamic_slice_in_dim(rank_table, seq, 1, 0).reshape(-1)
    pos = my_owner * most + my_rank
    ids = seq * blocks + jnp.arange(blocks, dtype=jnp.int32)
    near = ids[:, None] + jnp.arange(-1, 2, dtype=jnp.int32)[None, :]
    far = (my_owner * blocks + my_slot).reshape(blocks, RND)
    okay = jnp.concatenate(
        [
            (near >= G) & (near <= n_seq * blocks - 1),
            (far >= G) & (jnp.abs(far - ids[:, None]) >= 2),
        ],
        axis=1,
    )
    bias = jnp.where(okay, 0.0, 1e30).astype(F32).reshape(-1)

    back = jnp.sum(
        jnp.where(
            pos[None, :] == jnp.arange(n_seq * most, dtype=jnp.int32)[:, None],
            jnp.arange(per_row, dtype=jnp.int32)[None, :],
            0,
        ),
        axis=1,
    )
    slots = n_seq * most
    step = BLK * group
    dq_all, kv_all = pl.pallas_call(
        functools.partial(fused, n_seq, n_head, most, blocks),
        out_shape=[
            jax.ShapeDtypeStruct((n_head, rows, HD), BF16),
            jax.ShapeDtypeStruct((n_head, 2, toks, HD), BF16),
        ],
        in_specs=[smem] * 5 + [hbm, hbm, vmem, vmem],
        out_specs=[vmem, vmem],
        scratch_shapes=[
            pltpu.VMEM((n_head * rows, HD), BF16),
            pltpu.VMEM((n_head * rows, HD), BF16),
            pltpu.VMEM((2, n_head * rows // 128, 1, 128), F32),
            pltpu.VMEM((2, span + 2 * BLK, HD), BF16),
            pltpu.VMEM((2, G * BLK, HD), BF16),
            pltpu.VMEM((slots, 2, BLK, HD), BF16),
            pltpu.VMEM((slots, 2, BLK, HD), BF16),
            pltpu.VMEM((blocks, 2, BLK, HD), BF16),
            pltpu.VMEM((2, span + 2 * BLK, HD), F32),
            pltpu.VMEM((2, G * BLK, HD), F32),
            pltpu.VMEM((blocks, HD, step), F32),
            pltpu.VMEM((n_head * rows, HD), BF16),
            pltpu.VMEM((per_row, 2, BLK, HD), BF16),
            pltpu.VMEM((slots, 2, BLK, HD), BF16),
            pltpu.VMEM((2, 2, BLK, HD), BF16),
            pltpu.VMEM((2, 2, BLK, HD), BF16),
            pltpu.VMEM((2, G * BLK, HD), BF16),
            pltpu.VMEM((n_seq, 2, G * BLK, HD), BF16),
            pltpu.VMEM((2, span, HD), BF16),
            dma((6, n_head)), dma((6, n_head)), dma((6,)),
            dma((n_seq,)), dma((n_seq,)), dma((4,)), dma((4,)), dma((n_seq,)), dma((n_seq,)),
            dma((n_seq,)), dma((n_seq,)),
        ],
        compiler_params=pltpu.CompilerParams(
            collective_id=0, has_side_effects=True, vmem_limit_bytes=60 << 20
        ),
        name="fused",
    )(jnp.maximum(pick, 0), pos, back, bias, share, by_head(queries), by_head(output_grad), kv, ld)

    query_grad = jnp.transpose(
        dq_all.reshape(n_head, toks, group, HD), (1, 0, 2, 3)
    ).reshape(toks, heads, HD)
    key_grad = jnp.transpose(kv_all[:, 0], (1, 0, 2))
    value_grad = jnp.transpose(kv_all[:, 1], (1, 0, 2))
    return query_grad, key_grad, value_grad


def solution(mesh):
    wide = P(("seq", "head"), None, None)
    return jax.shard_map(
        functools.partial(per_device, mesh.shape["seq"], mesh.shape["head"]),
        mesh=mesh,
        in_specs=(wide, wide, wide, wide, wide, P(("seq", "head"), None), P(), P()),
        out_specs=(wide, wide, wide),
        check_vma=False,
    )
```

```python
import functools
import math

import jax
import jax.numpy as jnp
from jax import lax
from jax.experimental import pallas as pl
from jax.experimental.pallas import tpu as pltpu
from jax.sharding import PartitionSpec as P

HD = 128
BLK = 128
G = 2
RND = 3
MESH = pl.DeviceIdType.MESH
F32 = jnp.float32
BF16 = jnp.bfloat16
LOG2E = math.log2(math.e)


def greet(n_seq, n_head, seq, head):
    barrier = pltpu.get_barrier_semaphore()

    def to_head(d, c):
        pl.semaphore_signal(
            barrier, inc=1, device_id={"head": lax.rem(head + d, n_head)}, device_id_type=MESH
        )
        return c

    def to_seq(d, c):
        pl.semaphore_signal(
            barrier, inc=1, device_id={"seq": lax.rem(seq + d, n_seq)}, device_id_type=MESH
        )
        return c

    lax.fori_loop(1, n_head, to_head, 0)
    lax.fori_loop(1, n_seq, to_seq, 0)
    pl.semaphore_wait(barrier, n_head + n_seq - 2)


def remote(src, dst, send, recv, **where):
    return pltpu.make_async_remote_copy(
        src_ref=src,
        dst_ref=dst,
        send_sem=send,
        recv_sem=recv,
        device_id=where,
        device_id_type=MESH,
    )


def dot(a, b, ca, cb):
    return lax.dot_general(a, b, (((ca,), (cb,)), ((), ())), preferred_element_type=F32)


def pair_grads(k, v, shifts, q, g, delta, scaling):
    scores = dot(k, q, 1, 1) * (scaling * LOG2E)
    weights = jnp.concatenate(
        [jnp.exp2(scores[i * BLK : (i + 1) * BLK] - shift) for i, shift in enumerate(shifts)],
        axis=0,
    )
    score_grad = (weights * (dot(v, g, 1, 1) - delta)).astype(BF16)
    dv = dot(weights.astype(BF16), g, 1, 0)
    dk = dot(score_grad, q, 1, 0) * scaling
    return dk, dv, dot(k, score_grad, 0, 0)


def fused(
    n_seq, n_head, most, blocks,
    pick, pos, back, bias, share, q_in, g_in, kv_in, ld_in,
    dq_out, kv_out,
    q_all, g_all, ld_all, kv_ext, glob, rand, picked, held, acc, gacc, dq_acc, dq_all,
    rpart, rback, halo_part, halo, gpart, gall, kv_sum,
    hs, hr, ls, ss, sr, ns, nr, gs, gr, rs, rr,
):
    seq, head = lax.axis_index("seq"), lax.axis_index("head")
    toks = kv_in.shape[2]
    group = q_in.shape[1] // n_head
    rows = toks * group
    span = n_head * toks
    lines = rows // 128
    step = rows * n_head // blocks
    scaling = 1.0 / HD**0.5
    greet(n_seq, n_head, seq, head)

    def partner(d):
        base = lax.rem(head + 2 * (d // 2), n_head)
        return base + (1 - 2 * lax.rem(base, 2)) if d % 2 else base

    mine = pl.ds(pl.multiple_of(head * rows, rows), rows)
    here = pl.ds(pl.multiple_of(head * toks, toks), toks)
    q_to = q_all.at[here]
    g_to = g_all.at[here]
    kv_to = kv_ext.at[:, pl.ds(pl.multiple_of(BLK + head * toks, 32), toks), :]
    ld_to = ld_all.at[:, pl.ds(head * lines, lines)]

    def heads_of(ref, peer):
        return ref.at[:, pl.ds(pl.multiple_of(peer * group, group), group), :]

    def head_copy(kind, d):
        peer = partner(d)
        src, dst = (
            (kv_in.at[peer], kv_to),
            (ld_in.at[peer], ld_to),
            (heads_of(q_in, peer), q_to),
            (heads_of(g_in, peer), g_to),
        )[kind]
        return remote(src, dst, hs.at[kind, d], hr.at[kind, d], head=peer)

    own = [
        pltpu.make_async_copy(kv_in.at[head], kv_to, ls.at[0]),
        pltpu.make_async_copy(ld_in.at[head], ld_to, ls.at[1]),
        pltpu.make_async_copy(heads_of(q_in, head), q_to, ls.at[2]),
        pltpu.make_async_copy(heads_of(g_in, head), g_to, ls.at[3]),
    ]
    for kind in range(4):
        own[kind].start()
    for kind in range(4):
        for d in list(range(2, n_head)) + [1]:
            head_copy(kind, d).start()
    own[0].wait()
    for d in range(1, n_head):
        head_copy(0, d).wait_recv()

    up, down = lax.rem(seq + 1, n_seq), lax.rem(seq + n_seq - 1, n_seq)
    to_up = remote(
        kv_ext.at[:, pl.ds(span, BLK), :], kv_ext.at[:, pl.ds(0, BLK), :],
        ns.at[0], nr.at[0], seq=up,
    )
    to_down = remote(
        kv_ext.at[:, pl.ds(BLK, BLK), :], kv_ext.at[:, pl.ds(BLK + span, BLK), :],
        ns.at[1], nr.at[1], seq=down,
    )

    def rand_copy(d):
        peer = lax.rem(seq + d, n_seq)
        return remote(
            picked.at[pl.ds(peer * most, most)], rand.at[pl.ds(seq * most, most)],
            ss.at[d], sr.at[d], seq=peer,
        )

    def glob_copy(d):
        return remote(kv_ext.at[:, pl.ds(BLK, G * BLK), :], glob, gs.at[d], gr.at[0], seq=d)

    def loop(low, high, body):
        def run(i, c):
            body(i)
            return c

        lax.fori_loop(low, high, run, 0)

    def fill(i):
        picked[i] = held[pick[i]]

    for block in range(blocks):
        held[block] = kv_ext[:, (block + 1) * BLK : (block + 2) * BLK, :]
    loop(0, n_seq * most, fill)
    to_up.start()
    to_down.start()

    @pl.when(seq == 0)
    def _():
        loop(1, n_seq, lambda d: glob_copy(d).start())
        glob[...] = kv_ext[:, BLK : BLK + G * BLK, :]

    loop(1, n_seq, lambda d: rand_copy(d).start())
    rand[pl.ds(seq * most, most)] = picked[pl.ds(seq * most, most)]

    acc[...] = jnp.zeros_like(acc)
    gacc[...] = jnp.zeros_like(gacc)
    to_up.wait()
    to_down.wait()

    @pl.when(seq > 0)
    def _():
        glob_copy(0).wait_recv()

    for kind in range(1, 4):
        own[kind].wait()
        head_copy(kind, 1).wait_recv()
    for d in range(2, n_head):
        head_copy(1, d).wait_recv()

    turn = head // (n_head // 2)

    def order(i):
        return i + turn * (blocks - 1 - 2 * i)

    def operands(b):
        spot = pl.ds(pl.multiple_of(b * BLK, BLK), BLK)
        per = step // 128

        def lanes(part):
            tile = ld_all[part, pl.ds(b * per, per)]
            return jnp.concatenate([tile[r] for r in range(per)], axis=1)

        flat = (step, HD)
        return q_all[spot].reshape(flat), g_all[spot].reshape(flat), lanes(0) * LOG2E, lanes(1)

    def near(i, fresh):
        b = order(i)
        q, g, lse, delta = operands(b)
        at = pl.multiple_of(b * BLK, BLK)
        win = pl.ds(at, 3 * BLK)
        dk, dv, dq = pair_grads(glob[0], glob[1], [lse] * G, q, g, delta, scaling)
        gacc[0] += dk
        gacc[1] += dv
        shifts = [lse + bias[b * (3 + RND) + j] for j in range(3)]
        dk, dv, more = pair_grads(kv_ext[0, win, :], kv_ext[1, win, :], shifts, q, g, delta, scaling)
        acc[0, win, :] += dk
        acc[1, win, :] += dv
        if fresh:
            dq_acc[b] = dq + more
        else:
            total = dq_acc[b] + dq + more
            dq_all[pl.ds(pl.multiple_of(b * step, step), step), :] = (total.T * scaling).astype(BF16)

    def far(i, fresh):
        b = order(i)
        q, g, lse, delta = operands(b)
        found = [rand[pos[b * RND + j]] for j in range(RND)]
        k = jnp.concatenate([f[0] for f in found], axis=0)
        v = jnp.concatenate([f[1] for f in found], axis=0)
        shifts = [lse + bias[b * (3 + RND) + 3 + j] for j in range(RND)]
        dk, dv, dq = pair_grads(k, v, shifts, q, g, delta, scaling)
        for j in range(RND):
            rpart[b * RND + j, 0] = dk[j * BLK : (j + 1) * BLK].astype(BF16)
            rpart[b * RND + j, 1] = dv[j * BLK : (j + 1) * BLK].astype(BF16)
        if fresh:
            dq_acc[b] = dq
        else:
            total = dq_acc[b] + dq
            dq_all[pl.ds(pl.multiple_of(b * step, step), step), :] = (total.T * scaling).astype(BF16)

    early = span // 2 // BLK
    loop(0, early, lambda i: near(i, True))
    loop(1, n_seq, lambda d: rand_copy(d).wait())
    loop(0, early, lambda i: far(i, False))
    for kind in range(2, 4):
        for d in range(2, n_head):
            head_copy(kind, d).wait_recv()
    loop(early, blocks, lambda i: far(i, True))

    def gather(i):
        picked[i] = rpart[back[i]]

    def back_copy(d):
        peer = lax.rem(seq + d, n_seq)
        return remote(
            picked.at[pl.ds(peer * most, most)], rback.at[pl.ds(seq * most, most)],
            rs.at[d], rr.at[d], seq=peer,
        )

    loop(0, n_seq * most, gather)
    rback[pl.ds(seq * most, most)] = picked[pl.ds(seq * most, most)]
    loop(1, n_seq, lambda d: back_copy(d).start())
    loop(early, blocks, lambda i: near(i, False))

    halo_part[0] = acc[:, 0:BLK, :].astype(BF16)
    halo_part[1] = acc[:, BLK + span :, :].astype(BF16)
    gpart[...] = gacc[...].astype(BF16)

    def dq_copy(d):
        peer = partner(d)
        src = dq_all.at[pl.ds(pl.multiple_of(peer * rows, rows), rows), :]
        return remote(src, dq_out.at[head], hs.at[4, d], hr.at[4, d], head=peer)

    def kv_copy(d):
        peer = partner(d)
        src = kv_sum.at[:, pl.ds(pl.multiple_of(peer * toks, 32), toks), :]
        return remote(src, kv_out.at[head], hs.at[5, d], hr.at[5, d], head=peer)

    def part_copy():
        return remote(gpart, gall.at[seq], gs.at[0], gr.at[seq], seq=0)

    down_grad = remote(halo_part.at[0], halo.at[0], ns.at[2], nr.at[2], seq=down)
    up_grad = remote(halo_part.at[1], halo.at[1], ns.at[3], nr.at[3], seq=up)
    own_dq = pltpu.make_async_copy(dq_all.at[mine, :], dq_out.at[head], ls.at[4])
    for d in list(range(2, n_head)) + [1]:
        dq_copy(d).start()
    own_dq.start()
    down_grad.start()
    up_grad.start()

    @pl.when(seq > 0)
    def _():
        part_copy().start()

    for kind in range(4):
        for d in range(1, n_head):
            head_copy(kind, d).wait_send()

    @pl.when(seq == 0)
    def _():
        loop(1, n_seq, lambda d: glob_copy(d).wait_send())
        gall[0] = gpart[...]

        def arrive(d):
            remote(gpart, gall.at[d], gs.at[0], gr.at[d], seq=0).wait_recv()

        loop(1, n_seq, arrive)

        def add(d):
            gacc[...] += gall[d].astype(F32)

        loop(1, n_seq, add)
        acc[:, BLK : BLK + G * BLK, :] += gacc[...]

    @pl.when(seq > 0)
    def _():
        part_copy().wait_send()

    down_grad.wait()
    up_grad.wait()
    acc[:, BLK : 2 * BLK, :] += halo[1].astype(F32)
    acc[:, span : span + BLK, :] += halo[0].astype(F32)
    def absorb(d):
        base = lax.rem(seq + n_seq - d, n_seq) * most

        def block_sum(block):
            over = pl.ds(pl.multiple_of(block * BLK + BLK, BLK), BLK)
            for part in range(2):
                value = acc[part, over, :]
                for m in range(most):
                    value = value + share[block, base + m] * rback[base + m, part].astype(F32)
                acc[part, over, :] = value

        loop(0, blocks, block_sum)

    def take(d):
        back_copy(d).wait()
        absorb(d)

    absorb(0)
    loop(1, n_seq, take)
    kv_sum[...] = acc[:, BLK : BLK + span, :].astype(BF16)
    own_kv = pltpu.make_async_copy(
        kv_sum.at[:, pl.ds(pl.multiple_of(head * toks, 32), toks), :], kv_out.at[head], ls.at[5]
    )
    for d in list(range(2, n_head)) + [1]:
        kv_copy(d).start()
    own_kv.start()
    own_dq.wait()
    for d in range(1, n_head):
        dq_copy(d).wait()
    own_kv.wait()
    for d in range(1, n_head):
        kv_copy(d).wait()


def per_device(
    n_seq, n_head,
    queries, key_states, value_states, outputs, output_grad, logsumexp, random_owner, random_slot,
):
    toks, heads, _ = queries.shape
    group = heads // n_head
    rows = toks * group
    span = toks * n_head
    blocks = span // BLK
    per_row = blocks * RND
    most = max(1, (per_row + n_seq - 1) // n_seq)
    seq = lax.axis_index("seq")
    vmem = pl.BlockSpec(memory_space=pltpu.VMEM)
    smem = pl.BlockSpec(memory_space=pltpu.SMEM)
    hbm = pl.BlockSpec(memory_space=pl.ANY)
    dma = pltpu.SemaphoreType.DMA

    delta = jnp.sum(output_grad.astype(F32) * outputs.astype(F32), axis=-1)

    ld = jnp.stack([logsumexp, delta]).reshape(2, toks, n_head, group)
    ld = jnp.transpose(ld, (2, 0, 1, 3)).reshape(n_head, 2, rows // 128, 1, 128)
    kv = jnp.transpose(jnp.stack([key_states, value_states]), (2, 0, 1, 3))

    owner_table = random_owner.reshape(n_seq, per_row)
    slot_table = random_slot.reshape(n_seq, per_row)
    entry = jnp.arange(per_row, dtype=jnp.int32)
    rank_table = jnp.sum(
        (
            (owner_table[:, :, None] == owner_table[:, None, :])
            & (entry[None, :] < entry[:, None])[None]
        ).astype(jnp.int32),
        axis=2,
    )
    hits = (owner_table == seq)[:, :, None] & (
        rank_table[:, :, None] == jnp.arange(most, dtype=jnp.int32)
    )
    pick = jnp.sum(jnp.where(hits, slot_table[:, :, None] + 1, 0), axis=1).reshape(-1) - 1
    share = (pick[None, :] == jnp.arange(blocks, dtype=jnp.int32)[:, None]).astype(F32)
    my_owner = lax.dynamic_slice_in_dim(owner_table, seq, 1, 0).reshape(-1)
    my_slot = lax.dynamic_slice_in_dim(slot_table, seq, 1, 0).reshape(-1)
    my_rank = lax.dynamic_slice_in_dim(rank_table, seq, 1, 0).reshape(-1)
    pos = my_owner * most + my_rank
    ids = seq * blocks + jnp.arange(blocks, dtype=jnp.int32)
    near = ids[:, None] + jnp.arange(-1, 2, dtype=jnp.int32)[None, :]
    far = (my_owner * blocks + my_slot).reshape(blocks, RND)
    okay = jnp.concatenate(
        [
            (near >= G) & (near <= n_seq * blocks - 1),
            (far >= G) & (jnp.abs(far - ids[:, None]) >= 2),
        ],
        axis=1,
    )
    bias = jnp.where(okay, 0.0, 1e30).astype(F32).reshape(-1)

    back = jnp.sum(
        jnp.where(
            pos[None, :] == jnp.arange(n_seq * most, dtype=jnp.int32)[:, None],
            jnp.arange(per_row, dtype=jnp.int32)[None, :],
            0,
        ),
        axis=1,
    )
    slots = n_seq * most
    step = BLK * group
    dq_all, kv_all = pl.pallas_call(
        functools.partial(fused, n_seq, n_head, most, blocks),
        out_shape=[
            jax.ShapeDtypeStruct((n_head, rows, HD), BF16),
            jax.ShapeDtypeStruct((n_head, 2, toks, HD), BF16),
        ],
        in_specs=[smem] * 5 + [hbm, hbm, vmem, vmem],
        out_specs=[vmem, vmem],
        scratch_shapes=[
            pltpu.VMEM((span, group, HD), BF16),
            pltpu.VMEM((span, group, HD), BF16),
            pltpu.VMEM((2, n_head * rows // 128, 1, 128), F32),
            pltpu.VMEM((2, span + 2 * BLK, HD), BF16),
            pltpu.VMEM((2, G * BLK, HD), BF16),
            pltpu.VMEM((slots, 2, BLK, HD), BF16),
            pltpu.VMEM((slots, 2, BLK, HD), BF16),
            pltpu.VMEM((blocks, 2, BLK, HD), BF16),
            pltpu.VMEM((2, span + 2 * BLK, HD), F32),
            pltpu.VMEM((2, G * BLK, HD), F32),
            pltpu.VMEM((blocks, HD, step), F32),
            pltpu.VMEM((n_head * rows, HD), BF16),
            pltpu.VMEM((per_row, 2, BLK, HD), BF16),
            pltpu.VMEM((slots, 2, BLK, HD), BF16),
            pltpu.VMEM((2, 2, BLK, HD), BF16),
            pltpu.VMEM((2, 2, BLK, HD), BF16),
            pltpu.VMEM((2, G * BLK, HD), BF16),
            pltpu.VMEM((n_seq, 2, G * BLK, HD), BF16),
            pltpu.VMEM((2, span, HD), BF16),
            dma((6, n_head)), dma((6, n_head)), dma((6,)),
            dma((n_seq,)), dma((n_seq,)), dma((4,)), dma((4,)), dma((n_seq,)), dma((n_seq,)),
            dma((n_seq,)), dma((n_seq,)),
        ],
        compiler_params=pltpu.CompilerParams(
            collective_id=0, has_side_effects=True, vmem_limit_bytes=60 << 20
        ),
        name="fused",
    )(jnp.maximum(pick, 0), pos, back, bias, share, queries, output_grad, kv, ld)

    query_grad = jnp.transpose(
        dq_all.reshape(n_head, toks, group, HD), (1, 0, 2, 3)
    ).reshape(toks, heads, HD)
    key_grad = jnp.transpose(kv_all[:, 0], (1, 0, 2))
    value_grad = jnp.transpose(kv_all[:, 1], (1, 0, 2))
    return query_grad, key_grad, value_grad


def solution(mesh):
    wide = P(("seq", "head"), None, None)
    return jax.shard_map(
        functools.partial(per_device, mesh.shape["seq"], mesh.shape["head"]),
        mesh=mesh,
        in_specs=(wide, wide, wide, wide, wide, P(("seq", "head"), None), P(), P()),
        out_specs=(wide, wide, wide),
        check_vma=False,
    )
```

```python
import functools
import math

import jax
import jax.numpy as jnp
from jax import lax
from jax.experimental import pallas as pl
from jax.experimental.pallas import tpu as pltpu
from jax.sharding import PartitionSpec as P

HD = 128
BLK = 128
G = 2
RND = 3
MESH = pl.DeviceIdType.MESH
F32 = jnp.float32
BF16 = jnp.bfloat16
LOG2E = math.log2(math.e)


def greet(n_seq, n_head, seq, head):
    barrier = pltpu.get_barrier_semaphore()

    def to_head(d, c):
        pl.semaphore_signal(
            barrier, inc=1, device_id={"head": lax.rem(head + d, n_head)}, device_id_type=MESH
        )
        return c

    def to_seq(d, c):
        pl.semaphore_signal(
            barrier, inc=1, device_id={"seq": lax.rem(seq + d, n_seq)}, device_id_type=MESH
        )
        return c

    lax.fori_loop(1, n_head, to_head, 0)
    lax.fori_loop(1, n_seq, to_seq, 0)
    pl.semaphore_wait(barrier, n_head + n_seq - 2)


def remote(src, dst, send, recv, **where):
    return pltpu.make_async_remote_copy(
        src_ref=src,
        dst_ref=dst,
        send_sem=send,
        recv_sem=recv,
        device_id=where,
        device_id_type=MESH,
    )


def dot(a, b, ca, cb):
    return lax.dot_general(a, b, (((ca,), (cb,)), ((), ())), preferred_element_type=F32)


def pair_grads(k, v, shifts, q, g, delta, scaling):
    scores = dot(k, q, 1, 1) * (scaling * LOG2E)
    weights = jnp.concatenate(
        [jnp.exp2(scores[i * BLK : (i + 1) * BLK] - shift) for i, shift in enumerate(shifts)],
        axis=0,
    )
    score_grad = (weights * (dot(v, g, 1, 1) - delta)).astype(BF16)
    dv = dot(weights.astype(BF16), g, 1, 0)
    dk = dot(score_grad, q, 1, 0) * scaling
    return dk, dv, dot(k, score_grad, 0, 0)


def fused(
    n_seq, n_head, most, blocks,
    pick, pos, back, bias, share, q_in, g_in, kv_in, ld_in,
    dq_out, kv_out,
    q_all, g_all, ld_all, kv_ext, glob, rand, picked, held, acc, gacc, dq_acc, dq_all,
    rpart, rback, halo_part, halo, gpart, gall, kv_sum,
    hs, hr, ls, ss, sr, ns, nr, gs, gr, rs, rr,
):
    seq, head = lax.axis_index("seq"), lax.axis_index("head")
    toks = kv_in.shape[2]
    group = q_in.shape[1] // n_head
    rows = toks * group
    span = n_head * toks
    lines = rows // 128
    step = rows * n_head // blocks
    scaling = 1.0 / HD**0.5
    greet(n_seq, n_head, seq, head)

    def partner(d):
        base = lax.rem(head + 2 * (d // 2), n_head)
        return base + (1 - 2 * lax.rem(base, 2)) if d % 2 else base

    here = pl.ds(pl.multiple_of(head * toks, toks), toks)
    q_to = q_all.at[here]
    g_to = g_all.at[here]
    kv_to = kv_ext.at[:, pl.ds(pl.multiple_of(BLK + head * toks, 32), toks), :]
    ld_to = ld_all.at[:, pl.ds(head * lines, lines)]

    def heads_of(ref, peer):
        return ref.at[:, pl.ds(pl.multiple_of(peer * group, group), group), :]

    def head_copy(kind, d):
        peer = partner(d)
        src, dst = (
            (kv_in.at[peer], kv_to),
            (ld_in.at[peer], ld_to),
            (heads_of(q_in, peer), q_to),
            (heads_of(g_in, peer), g_to),
        )[kind]
        return remote(src, dst, hs.at[kind, d], hr.at[kind, d], head=peer)

    own = [
        pltpu.make_async_copy(kv_in.at[head], kv_to, ls.at[0]),
        pltpu.make_async_copy(ld_in.at[head], ld_to, ls.at[1]),
        pltpu.make_async_copy(heads_of(q_in, head), q_to, ls.at[2]),
        pltpu.make_async_copy(heads_of(g_in, head), g_to, ls.at[3]),
    ]
    for kind in range(4):
        own[kind].start()
    for kind in range(4):
        for d in list(range(2, n_head)) + [1]:
            head_copy(kind, d).start()
    own[0].wait()
    for d in range(1, n_head):
        head_copy(0, d).wait_recv()

    up, down = lax.rem(seq + 1, n_seq), lax.rem(seq + n_seq - 1, n_seq)
    to_up = remote(
        kv_ext.at[:, pl.ds(span, BLK), :], kv_ext.at[:, pl.ds(0, BLK), :],
        ns.at[0], nr.at[0], seq=up,
    )
    to_down = remote(
        kv_ext.at[:, pl.ds(BLK, BLK), :], kv_ext.at[:, pl.ds(BLK + span, BLK), :],
        ns.at[1], nr.at[1], seq=down,
    )

    def rand_copy(d):
        peer = lax.rem(seq + d, n_seq)
        return remote(
            picked.at[pl.ds(peer * most, most)], rand.at[pl.ds(seq * most, most)],
            ss.at[d], sr.at[d], seq=peer,
        )

    def glob_copy(d):
        return remote(kv_ext.at[:, pl.ds(BLK, G * BLK), :], glob, gs.at[d], gr.at[0], seq=d)

    def loop(low, high, body):
        def run(i, c):
            body(i)
            return c

        lax.fori_loop(low, high, run, 0)

    def fill(i):
        picked[i] = held[pick[i]]

    for block in range(blocks):
        held[block] = kv_ext[:, (block + 1) * BLK : (block + 2) * BLK, :]
    loop(0, n_seq * most, fill)
    to_up.start()
    to_down.start()

    @pl.when(seq == 0)
    def _():
        loop(1, n_seq, lambda d: glob_copy(d).start())
        glob[...] = kv_ext[:, BLK : BLK + G * BLK, :]

    loop(1, n_seq, lambda d: rand_copy(d).start())
    rand[pl.ds(seq * most, most)] = picked[pl.ds(seq * most, most)]

    acc[...] = jnp.zeros_like(acc)
    gacc[...] = jnp.zeros_like(gacc)
    to_up.wait()
    to_down.wait()

    @pl.when(seq > 0)
    def _():
        glob_copy(0).wait_recv()

    for kind in range(1, 4):
        own[kind].wait()
        head_copy(kind, 1).wait_recv()
    for d in range(2, n_head):
        head_copy(1, d).wait_recv()

    turn = head // (n_head // 2)

    def order(i):
        return i + turn * (blocks - 1 - 2 * i)

    def operands(b):
        spot = pl.ds(pl.multiple_of(b * BLK, BLK), BLK)
        per = step // 128

        def lanes(part):
            tile = ld_all[part, pl.ds(b * per, per)]
            return jnp.concatenate([tile[r] for r in range(per)], axis=1)

        flat = (step, HD)
        return q_all[spot].reshape(flat), g_all[spot].reshape(flat), lanes(0) * LOG2E, lanes(1)

    def near(i, fresh):
        b = order(i)
        q, g, lse, delta = operands(b)
        at = pl.multiple_of(b * BLK, BLK)
        win = pl.ds(at, 3 * BLK)
        dk, dv, dq = pair_grads(glob[0], glob[1], [lse] * G, q, g, delta, scaling)
        gacc[0] += dk
        gacc[1] += dv
        shifts = [lse + bias[b * (3 + RND) + j] for j in range(3)]
        dk, dv, more = pair_grads(kv_ext[0, win, :], kv_ext[1, win, :], shifts, q, g, delta, scaling)
        acc[0, win, :] += dk
        acc[1, win, :] += dv
        if fresh:
            dq_acc[b] = dq + more
        else:
            total = dq_acc[b] + dq + more
            dq_all[pl.ds(at, BLK)] = (total.T * scaling).astype(BF16).reshape(BLK, group, HD)

    def far(i, fresh):
        b = order(i)
        q, g, lse, delta = operands(b)
        at = pl.multiple_of(b * BLK, BLK)
        found = [rand[pos[b * RND + j]] for j in range(RND)]
        k = jnp.concatenate([f[0] for f in found], axis=0)
        v = jnp.concatenate([f[1] for f in found], axis=0)
        shifts = [lse + bias[b * (3 + RND) + 3 + j] for j in range(RND)]
        dk, dv, dq = pair_grads(k, v, shifts, q, g, delta, scaling)
        for j in range(RND):
            rpart[b * RND + j, 0] = dk[j * BLK : (j + 1) * BLK].astype(BF16)
            rpart[b * RND + j, 1] = dv[j * BLK : (j + 1) * BLK].astype(BF16)
        if fresh:
            dq_acc[b] = dq
        else:
            total = dq_acc[b] + dq
            dq_all[pl.ds(at, BLK)] = (total.T * scaling).astype(BF16).reshape(BLK, group, HD)

    early = span // 2 // BLK
    loop(0, early, lambda i: near(i, True))
    loop(1, n_seq, lambda d: rand_copy(d).wait())
    loop(0, early, lambda i: far(i, False))
    for kind in range(2, 4):
        for d in range(2, n_head):
            head_copy(kind, d).wait_recv()
    loop(early, blocks, lambda i: far(i, True))

    def gather(i):
        picked[i] = rpart[back[i]]

    def back_copy(d):
        peer = lax.rem(seq + d, n_seq)
        return remote(
            picked.at[pl.ds(peer * most, most)], rback.at[pl.ds(seq * most, most)],
            rs.at[d], rr.at[d], seq=peer,
        )

    loop(0, n_seq * most, gather)
    rback[pl.ds(seq * most, most)] = picked[pl.ds(seq * most, most)]
    loop(1, n_seq, lambda d: back_copy(d).start())
    loop(early, blocks, lambda i: near(i, False))

    halo_part[0] = acc[:, 0:BLK, :].astype(BF16)
    halo_part[1] = acc[:, BLK + span :, :].astype(BF16)
    gpart[...] = gacc[...].astype(BF16)

    def dq_copy(d):
        peer = partner(d)
        src = dq_all.at[pl.ds(pl.multiple_of(peer * toks, toks), toks)]
        return remote(src, heads_of(dq_out, head), hs.at[4, d], hr.at[4, d], head=peer)

    def kv_copy(d):
        peer = partner(d)
        src = kv_sum.at[:, pl.ds(pl.multiple_of(peer * toks, 32), toks), :]
        return remote(src, kv_out.at[head], hs.at[5, d], hr.at[5, d], head=peer)

    def part_copy():
        return remote(gpart, gall.at[seq], gs.at[0], gr.at[seq], seq=0)

    down_grad = remote(halo_part.at[0], halo.at[0], ns.at[2], nr.at[2], seq=down)
    up_grad = remote(halo_part.at[1], halo.at[1], ns.at[3], nr.at[3], seq=up)
    own_dq = pltpu.make_async_copy(dq_all.at[here], heads_of(dq_out, head), ls.at[4])
    for d in list(range(2, n_head)) + [1]:
        dq_copy(d).start()
    own_dq.start()
    down_grad.start()
    up_grad.start()

    @pl.when(seq > 0)
    def _():
        part_copy().start()

    for kind in range(4):
        for d in range(1, n_head):
            head_copy(kind, d).wait_send()

    @pl.when(seq == 0)
    def _():
        loop(1, n_seq, lambda d: glob_copy(d).wait_send())
        gall[0] = gpart[...]

        def arrive(d):
            remote(gpart, gall.at[d], gs.at[0], gr.at[d], seq=0).wait_recv()

        loop(1, n_seq, arrive)

        def add(d):
            gacc[...] += gall[d].astype(F32)

        loop(1, n_seq, add)
        acc[:, BLK : BLK + G * BLK, :] += gacc[...]

    @pl.when(seq > 0)
    def _():
        part_copy().wait_send()

    down_grad.wait()
    up_grad.wait()
    acc[:, BLK : 2 * BLK, :] += halo[1].astype(F32)
    acc[:, span : span + BLK, :] += halo[0].astype(F32)
    def absorb(d):
        base = lax.rem(seq + n_seq - d, n_seq) * most

        def block_sum(block):
            over = pl.ds(pl.multiple_of(block * BLK + BLK, BLK), BLK)
            for part in range(2):
                value = acc[part, over, :]
                for m in range(most):
                    value = value + share[block, base + m] * rback[base + m, part].astype(F32)
                acc[part, over, :] = value

        loop(0, blocks, block_sum)

    def take(d):
        back_copy(d).wait()
        absorb(d)

    absorb(0)
    loop(1, n_seq, take)
    kv_sum[...] = acc[:, BLK : BLK + span, :].astype(BF16)
    own_kv = pltpu.make_async_copy(
        kv_sum.at[:, pl.ds(pl.multiple_of(head * toks, 32), toks), :], kv_out.at[head], ls.at[5]
    )
    for d in list(range(2, n_head)) + [1]:
        kv_copy(d).start()
    own_kv.start()
    own_dq.wait()
    for d in range(1, n_head):
        dq_copy(d).wait()
    own_kv.wait()
    for d in range(1, n_head):
        kv_copy(d).wait()


def per_device(
    n_seq, n_head,
    queries, key_states, value_states, outputs, output_grad, logsumexp, random_owner, random_slot,
):
    toks, heads, _ = queries.shape
    group = heads // n_head
    rows = toks * group
    span = toks * n_head
    blocks = span // BLK
    per_row = blocks * RND
    most = max(1, (per_row + n_seq - 1) // n_seq)
    seq = lax.axis_index("seq")
    vmem = pl.BlockSpec(memory_space=pltpu.VMEM)
    smem = pl.BlockSpec(memory_space=pltpu.SMEM)
    hbm = pl.BlockSpec(memory_space=pl.ANY)
    dma = pltpu.SemaphoreType.DMA

    delta = jnp.sum(output_grad.astype(F32) * outputs.astype(F32), axis=-1)

    ld = jnp.stack([logsumexp, delta]).reshape(2, toks, n_head, group)
    ld = jnp.transpose(ld, (2, 0, 1, 3)).reshape(n_head, 2, rows // 128, 1, 128)
    kv = jnp.transpose(jnp.stack([key_states, value_states]), (2, 0, 1, 3))

    owner_table = random_owner.reshape(n_seq, per_row)
    slot_table = random_slot.reshape(n_seq, per_row)
    entry = jnp.arange(per_row, dtype=jnp.int32)
    rank_table = jnp.sum(
        (
            (owner_table[:, :, None] == owner_table[:, None, :])
            & (entry[None, :] < entry[:, None])[None]
        ).astype(jnp.int32),
        axis=2,
    )
    hits = (owner_table == seq)[:, :, None] & (
        rank_table[:, :, None] == jnp.arange(most, dtype=jnp.int32)
    )
    pick = jnp.sum(jnp.where(hits, slot_table[:, :, None] + 1, 0), axis=1).reshape(-1) - 1
    share = (pick[None, :] == jnp.arange(blocks, dtype=jnp.int32)[:, None]).astype(F32)
    my_owner = lax.dynamic_slice_in_dim(owner_table, seq, 1, 0).reshape(-1)
    my_slot = lax.dynamic_slice_in_dim(slot_table, seq, 1, 0).reshape(-1)
    my_rank = lax.dynamic_slice_in_dim(rank_table, seq, 1, 0).reshape(-1)
    pos = my_owner * most + my_rank
    ids = seq * blocks + jnp.arange(blocks, dtype=jnp.int32)
    near = ids[:, None] + jnp.arange(-1, 2, dtype=jnp.int32)[None, :]
    far = (my_owner * blocks + my_slot).reshape(blocks, RND)
    okay = jnp.concatenate(
        [
            (near >= G) & (near <= n_seq * blocks - 1),
            (far >= G) & (jnp.abs(far - ids[:, None]) >= 2),
        ],
        axis=1,
    )
    bias = jnp.where(okay, 0.0, 1e30).astype(F32).reshape(-1)

    back = jnp.sum(
        jnp.where(
            pos[None, :] == jnp.arange(n_seq * most, dtype=jnp.int32)[:, None],
            jnp.arange(per_row, dtype=jnp.int32)[None, :],
            0,
        ),
        axis=1,
    )
    slots = n_seq * most
    step = BLK * group
    query_grad, kv_all = pl.pallas_call(
        functools.partial(fused, n_seq, n_head, most, blocks),
        out_shape=[
            jax.ShapeDtypeStruct((toks, heads, HD), BF16),
            jax.ShapeDtypeStruct((n_head, 2, toks, HD), BF16),
        ],
        in_specs=[smem] * 5 + [hbm, hbm, vmem, vmem],
        out_specs=[hbm, vmem],
        scratch_shapes=[
            pltpu.VMEM((span, group, HD), BF16),
            pltpu.VMEM((span, group, HD), BF16),
            pltpu.VMEM((2, n_head * rows // 128, 1, 128), F32),
            pltpu.VMEM((2, span + 2 * BLK, HD), BF16),
            pltpu.VMEM((2, G * BLK, HD), BF16),
            pltpu.VMEM((slots, 2, BLK, HD), BF16),
            pltpu.VMEM((slots, 2, BLK, HD), BF16),
            pltpu.VMEM((blocks, 2, BLK, HD), BF16),
            pltpu.VMEM((2, span + 2 * BLK, HD), F32),
            pltpu.VMEM((2, G * BLK, HD), F32),
            pltpu.VMEM((blocks, HD, step), F32),
            pltpu.VMEM((span, group, HD), BF16),
            pltpu.VMEM((per_row, 2, BLK, HD), BF16),
            pltpu.VMEM((slots, 2, BLK, HD), BF16),
            pltpu.VMEM((2, 2, BLK, HD), BF16),
            pltpu.VMEM((2, 2, BLK, HD), BF16),
            pltpu.VMEM((2, G * BLK, HD), BF16),
            pltpu.VMEM((n_seq, 2, G * BLK, HD), BF16),
            pltpu.VMEM((2, span, HD), BF16),
            dma((6, n_head)), dma((6, n_head)), dma((6,)),
            dma((n_seq,)), dma((n_seq,)), dma((4,)), dma((4,)), dma((n_seq,)), dma((n_seq,)),
            dma((n_seq,)), dma((n_seq,)),
        ],
        compiler_params=pltpu.CompilerParams(
            collective_id=0, has_side_effects=True, vmem_limit_bytes=60 << 20
        ),
        name="fused",
    )(jnp.maximum(pick, 0), pos, back, bias, share, queries, output_grad, kv, ld)

    key_grad = jnp.transpose(kv_all[:, 0], (1, 0, 2))
    value_grad = jnp.transpose(kv_all[:, 1], (1, 0, 2))
    return query_grad, key_grad, value_grad


def solution(mesh):
    wide = P(("seq", "head"), None, None)
    return jax.shard_map(
        functools.partial(per_device, mesh.shape["seq"], mesh.shape["head"]),
        mesh=mesh,
        in_specs=(wide, wide, wide, wide, wide, P(("seq", "head"), None), P(), P()),
        out_specs=(wide, wide, wide),
        check_vma=False,
    )
```
